32 devices in a mesh: groups: 2 (over x), rows: 8 (over z, y), fsdp: 2 (over core).
Axes of the slice: x: 2, y: 2, z: 4, core: 2. Of those that a mesh axis runs over, the one named last changes fastest.
Arguments:
- image: bfloat16 [32, 256, 512], P(('groups', 'rows'), 'fsdp'), parts along dimension 0, may hold values from -81 to 81
- deconv_weight: bfloat16 [4, 4, 512, 256], P(None, None, None, 'fsdp'), may hold values from -0.125 to 0.125
- norm_gain: float32 [256], replicated, may hold values from 0.1 to 1.9
- norm_shift: float32 [256], replicated, may hold values from -3 to 3
- first_weight: bfloat16 [3, 3, 256, 256], P(None, None, None, 'fsdp'), may hold values from -0.125 to 0.125
- first_bias: float32 [256], replicated, may hold values from -3 to 3
- second_weight: bfloat16 [3, 3, 256, 256], P(None, None, None, 'fsdp'), may hold values from -0.125 to 0.125
- second_bias: float32 [256], replicated, may hold values from -3 to 3
Outputs:
- result: bfloat16 [64, 512, 256], P(('groups', 'rows'), 'fsdp'), parts along dimension 0
The draws below stay inside these ranges and needn't reach their ends.
There are 2 independent parts, one for each index of `groups`. The reference program is written for one: setup_inputs(seed, part) draws one part's arguments, and reference() takes and returns one part's arrays. A program takes and returns all parts, laid end to end along the dimension named above; an argument that names none is the same for every part. Nothing has to cross between parts.
All inputs are finite; a program needn't handle non-finite values.
Results may differ from the reference program's by a relative error of at most 0.0055.
Values may be sent and summed in bfloat16 or wider, within the bound.
A program may use at most 64 MiB of HBM per device.

```python
import jax
import jax.numpy as jnp
from jax import lax

CIN = 512
COUT = 256
NORM_GROUPS = 32
IN_ROWS = 16
IN_COLS = 256


def draw_image(key, part):
    first_key, second_key = jax.random.split(key, 2)
    position = jnp.arange(IN_ROWS, dtype=jnp.float32) / max(IN_ROWS - 1, 1)
    offset = jax.random.uniform(second_key, (CIN,), jnp.float32, -1.0, 1.0)
    base = jnp.clip(jax.random.normal(first_key, (IN_ROWS, IN_COLS, CIN), jnp.float32), -6.0, 6.0)
    values = (base + offset) * (1.0 + 2.0 * position)[:, None, None]
    return values.astype(jnp.bfloat16)


def levels(own_key, dims, cuts, low, largest):
    def one(dim, blocks):
        heights = jax.random.uniform(jax.random.fold_in(jax.random.fold_in(own_key, 6), dim), (blocks,), jnp.float32, low / len(cuts), largest / len(cuts))
        return jnp.repeat(jnp.exp(heights), dims[dim] // blocks).reshape((-1,) + (1,) * (len(dims) - dim - 1))

    loudness = one(*cuts[0])
    for cut in cuts[1:]:
        loudness = loudness * one(*cut)
    return loudness


def bell_draw(key, extent, scale, bound, shards=(), kind=jnp.bfloat16):
    gain = levels(key, extent, shards, -0.22, 0.18) if shards else 1.0
    values = jax.random.normal(key, extent, jnp.float32) * scale * gain
    return jnp.minimum(jnp.maximum(values, -bound), bound).astype(kind)


def setup_inputs(seed: int = 0, part: int = 0) -> dict:
    splits = jax.random.split(jax.random.key(seed), 9)
    part_splits = jax.random.split(jax.random.fold_in(splits[8], part), 9)
    return {
        "image": draw_image(jax.random.fold_in(jax.random.fold_in(splits[8], part), 71), part),
        "deconv_weight": bell_draw(splits[1], (4, 4, CIN, COUT), (4 * CIN) ** -0.5, 0.125, ((3, 2),)),
        "norm_gain": jnp.clip(1.0 + 0.18 * jax.random.normal(splits[2], (COUT,), jnp.float32), 0.1, 1.9),
        "norm_shift": bell_draw(splits[3], (COUT,), 0.5, 3.0, (), jnp.float32),
        "first_weight": bell_draw(splits[4], (3, 3, COUT, COUT), (9 * COUT) ** -0.5, 0.125, ((3, 2),)),
        "first_bias": bell_draw(splits[5], (COUT,), 0.5, 3.0, (), jnp.float32),
        "second_weight": bell_draw(splits[6], (3, 3, COUT, COUT), (9 * COUT) ** -0.5, 0.125, ((3, 2),)),
        "second_bias": bell_draw(splits[7], (COUT,), 0.5, 3.0, (), jnp.float32),
    }


TAP_TABLE = (((0, 3), (1, 1)), ((1, 2), (2, 0)))

def upsample(padded, weight):
    height = padded.shape[0] - 2
    breadth = padded.shape[1] - 2
    inputs = padded.shape[2]
    outputs = weight.shape[3]
    phases = []
    for phase_row in range(2):
        line = []
        for phase_col in range(2):
            total = jnp.zeros((height * breadth, outputs), jnp.float32)
            for row_off, row_tap in TAP_TABLE[phase_row]:
                for col_off, col_tap in TAP_TABLE[phase_col]:
                    patch = padded[row_off:row_off + height, col_off:col_off + breadth].reshape(height * breadth, inputs)
                    total = total + jnp.dot(patch, weight[row_tap, col_tap], preferred_element_type=jnp.float32)
            line.append(total.reshape(height, breadth, outputs))
        phases.append(jnp.stack(line, axis=2))
    stacked = jnp.stack(phases, axis=1)
    return stacked.reshape(2 * height, 2 * breadth, outputs)

def convolve(padded, weight):
    height = padded.shape[0] - 2
    breadth = padded.shape[1] - 2
    inputs = padded.shape[2]
    outputs = weight.shape[3]
    total = jnp.zeros((height * breadth, outputs), jnp.float32)
    for row_tap in range(3):
        for col_tap in range(3):
            patch = padded[row_tap:row_tap + height, col_tap:col_tap + breadth].reshape(height * breadth, inputs)
            total = total + jnp.dot(patch, weight[row_tap, col_tap], preferred_element_type=jnp.float32)
    return total.reshape(height, breadth, outputs)

def reference(image, deconv_weight, norm_gain, norm_shift, first_weight, first_bias, second_weight, second_bias):
    padded = jnp.pad(image, ((1, 1), (1, 1), (0, 0)))
    upsampled = upsample(padded, deconv_weight).astype(jnp.bfloat16)
    values = upsampled.astype(jnp.float32)
    width = COUT // NORM_GROUPS
    grouped = values.reshape(-1, NORM_GROUPS, width)
    count = grouped.shape[0] * width
    mean = lax.optimization_barrier(jnp.sum(grouped, axis=(0, 2))) / count
    centered = grouped - mean[None, :, None]
    spread = lax.optimization_barrier(jnp.sum(centered * centered, axis=(0, 2))) / count
    scale = jnp.repeat(lax.rsqrt(spread + 1e-05), width) * norm_gain
    shift = norm_shift - jnp.repeat(mean, width) * scale
    hidden = jax.nn.silu(values * scale + shift).astype(jnp.bfloat16)
    first = convolve(jnp.pad(hidden, ((1, 1), (1, 1), (0, 0))), first_weight) + first_bias
    activated = jax.nn.silu(first).astype(jnp.bfloat16)
    second = convolve(jnp.pad(activated, ((1, 1), (1, 1), (0, 0))), second_weight) + second_bias
    return second.astype(jnp.bfloat16)
```

```python
import functools

import jax
import jax.numpy as jnp
from jax import lax
from jax.experimental import pallas as pl
from jax.experimental.pallas import tpu as pltpu
from jax.sharding import PartitionSpec as P

NORM_GROUPS = 32
EPS = 1e-05
MESH = pl.DeviceIdType.MESH
EDGE = 16
TAPS = ((3, 1), (2, 0))


def silu(v):
    h = 0.5 * v
    return h + h * jnp.tanh(h)


def kernel(
    rows, cores,
    image, dw, gain_in, shift_in, w1, b1_in, w2, b2_in,
    acts, w2buf, b2,
    gain, shift, b1,
    xbuf, xf, xs, dwbuf, w1buf, up, hf, hs, stats, same,
    local_sem, send_sem, recv_sem, stat_send, stat_recv, ring,
):
    row, core = lax.axis_index("rows"), lax.axis_index("fsdp")
    other = cores - 1 - core
    count = rows * cores
    me = row * cores + core
    height, breadth, cin = image.shape
    cout = gain.shape[1]
    half = dw.shape[1]
    span = xs.shape[1]
    side = pl.multiple_of(other * (breadth - EDGE), EDGE)
    far = pl.multiple_of(core * (breadth + EDGE), EDGE)
    mine = pl.multiple_of(core * half, 128)

    locals_ = [
        pltpu.make_async_copy(
            image, xbuf.at[pl.ds(height, height), pl.ds(EDGE, breadth)], local_sem.at[0]
        ),
        pltpu.make_async_copy(dw, dwbuf.at[:, pl.ds(mine, half)], local_sem.at[1]),
        pltpu.make_async_copy(w1, w1buf.at[:, pl.ds(mine, half)], local_sem.at[2]),
        pltpu.make_async_copy(w2, w2buf.at[:, pl.ds(mine, half)], local_sem.at[3]),
        pltpu.make_async_copy(gain_in, gain, local_sem.at[4]),
        pltpu.make_async_copy(shift_in, shift, local_sem.at[5]),
        pltpu.make_async_copy(b1_in, b1, local_sem.at[6]),
        pltpu.make_async_copy(b2_in, b2, local_sem.at[7]),
    ]

    barrier = pltpu.get_barrier_semaphore()

    def signal(sem, to_row, to_core):
        pl.semaphore_signal(
            sem, inc=1, device_id={"rows": to_row, "fsdp": to_core}, device_id_type=MESH
        )

    def call(sem, gap, to_cores):
        for inside, to_row in ((row >= gap, row - gap), (row + gap < rows, row + gap)):
            @pl.when(inside)
            def _():
                for to_core in to_cores:
                    signal(sem, to_row, to_core)
        near = jnp.where(row >= gap, 1, 0) + jnp.where(row + gap < rows, 1, 0)
        return near * len(to_cores)

    signal(barrier, row, other)
    met = call(barrier, 1, (core, other)) + 1
    for copy in locals_:
        copy.start()
    xbuf[:, pl.ds(far, EDGE), :] = jnp.zeros((xbuf.shape[0], EDGE, cin), xbuf.dtype)
    pl.semaphore_wait(barrier, met)

    def remote(src, dst, index, to_row, to_core):
        return pltpu.make_async_remote_copy(
            src_ref=src,
            dst_ref=dst,
            send_sem=send_sem.at[index],
            recv_sem=recv_sem.at[index],
            device_id={"rows": to_row, "fsdp": to_core},
            device_id_type=MESH,
        )

    def piece(src_row, dst_row, index, to_row, low, size):
        return remote(
            image.at[src_row, pl.ds(low, size)],
            xbuf.at[dst_row, pl.ds(EDGE + low, size)],
            index, to_row, core,
        )

    def corner(src_row, dst_row, index, to_row):
        return remote(
            image.at[src_row, pl.ds(side, EDGE)],
            xbuf.at[dst_row, pl.ds(far, EDGE)],
            index, to_row, other,
        )

    top, bottom = row == 0, row == rows - 1
    below = jnp.where(bottom, row - 1, row + 1)
    above = jnp.where(top, row + 1, row - 1)

    def pair(src_row, dst_row, index, to_row):
        return [
            piece(src_row, dst_row, index, to_row, 0, breadth),
            corner(src_row, dst_row, index + 1, to_row),
        ]

    down, up_ = pair(1, 1, 4, below), pair(0, 4, 6, above)
    last_down, first_up = pair(1, 5, 8, below), pair(0, 0, 10, above)
    reach = pl.multiple_of(other * EDGE, EDGE)

    def pass_on(src_row, dst_row, index, to_row):
        line = pl.ds(reach, breadth + EDGE)
        return remote(xbuf.at[src_row, line], xbuf.at[dst_row, line], index, to_row, core)

    relay_up = pass_on(1, 5, 12, lax.rem(row + rows - 2, rows))
    relay_down = pass_on(4, 0, 13, lax.rem(row + 2, rows))
    sides = remote(
        image.at[:, pl.ds(side, EDGE)],
        xbuf.at[pl.ds(height, height), pl.ds(far, EDGE)],
        0, row, other,
    )
    weights = [
        remote(dw, dwbuf.at[:, pl.ds(mine, half)], 1, row, other),
        remote(w1, w1buf.at[:, pl.ds(mine, half)], 2, row, other),
        remote(w2, w2buf.at[:, pl.ds(mine, half)], 3, row, other),
    ]

    def when(condition, copies, what):
        @pl.when(condition)
        def _():
            for copy in copies:
                getattr(copy, what)()

    def send_down():
        when(jnp.logical_not(bottom), down, "start")
        when(bottom, last_down, "start")

    def send_up():
        when(jnp.logical_not(top), up_, "start")
        when(top, first_up, "start")

    send_down()
    sides.start()
    weights[0].start()
    weights[1].start()
    weights[2].start()

    gaps = []
    while (1 << len(gaps)) < rows:
        gaps.append(1 << len(gaps))

    def meet(turn):
        pl.semaphore_wait(ring.at[turn], call(ring.at[turn], gaps[turn], (core,)))

    meet(0)

    @pl.when(row == 0)
    def _():
        xbuf[pl.ds(0, 2)] = jnp.zeros((2,) + xbuf.shape[1:], xbuf.dtype)

    @pl.when(row == rows - 1)
    def _():
        xbuf[pl.ds(4, 2)] = jnp.zeros((2,) + xbuf.shape[1:], xbuf.dtype)

    def spread_row(r):
        xf[...] = xbuf[r].astype(jnp.float32)
        xs[r, :, pl.ds(0, cin)] = xf[pl.ds(EDGE - 2, span), :].astype(jnp.bfloat16)
        xs[r, :, pl.ds(cin, cin)] = xf[pl.ds(EDGE - 1, span), :].astype(jnp.bfloat16)

    locals_[0].wait()
    sides.wait_recv()
    spread_row(2)
    spread_row(3)

    index = lax.broadcasted_iota(jnp.int32, (span, 1), 0)

    def upsample(pairs, phase_row, phase_col, measure):
        lhs = jnp.concatenate(
            [jnp.concatenate([xs[i], xs[i + 1]], axis=1) for _, i in pairs], axis=0
        )
        rhs = jnp.concatenate(
            [
                dwbuf[pl.ds((TAPS[phase_row][dr] * 4 + TAPS[phase_col][dc]) * cin, cin), :]
                for dr in range(2)
                for dc in range(2)
            ],
            axis=0,
        )
        total = jnp.dot(lhs, rhs, preferred_element_type=jnp.float32).astype(jnp.bfloat16)
        for n, (o, _) in enumerate(pairs):
            block = total[n * span : (n + 1) * span]
            up[o, phase_col] = block
            if measure is not False:
                first = 1 + phase_col
                own = (index >= first) & (index < first + breadth) & measure
                v = jnp.where(own, block.astype(jnp.float32), 0.0)
                stats[me, 0:1] += jnp.sum(v, axis=0, keepdims=True)
                stats[me, 1:2] += jnp.sum(v * v, axis=0, keepdims=True)

    stats[me] = jnp.zeros(stats.shape[1:], stats.dtype)
    width = cout // NORM_GROUPS
    lane_a = lax.broadcasted_iota(jnp.int32, (cout, cout), 0) // width
    lane_b = lax.broadcasted_iota(jnp.int32, (cout, cout), 1) // width
    same[...] = jnp.where(lane_a == lane_b, 1.0, 0.0).astype(jnp.bfloat16)
    locals_[1].wait()
    weights[0].wait_recv()
    send_up()
    for phase_col in range(2):
        upsample(((4, 2),), 0, phase_col, True)
        upsample(((3, 2),), 1, phase_col, True)

    @pl.when(bottom)
    def _():
        spread_row(4)
        for phase_col in range(2):
            upsample(((5, 3),), 1, phase_col, True)

    for turn in range(1, len(gaps)):
        meet(turn)

    when(jnp.logical_not(top), down, "wait_recv")
    spread_row(1)
    for phase_col in range(2):
        upsample(((2, 1),), 0, phase_col, True)
        upsample(((1, 1),), 1, phase_col, jnp.logical_not(top))

    def stat_copy(slot, peer):
        return pltpu.make_async_remote_copy(
            src_ref=stats.at[me],
            dst_ref=stats.at[me],
            send_sem=stat_send.at[slot],
            recv_sem=stat_recv.at[me],
            device_id={"rows": lax.div(peer, cores), "fsdp": lax.rem(peer, cores)},
            device_id_type=MESH,
        )

    def stat_wait(peer):
        return pltpu.make_async_remote_copy(
            src_ref=stats.at[peer],
            dst_ref=stats.at[peer],
            send_sem=stat_send.at[0],
            recv_sem=stat_recv.at[peer],
            device_id={"rows": lax.div(peer, cores), "fsdp": lax.rem(peer, cores)},
            device_id_type=MESH,
        )

    def send_stats(k, carry):
        stat_copy(k, lax.rem(me + k, count)).start()
        return carry

    lax.fori_loop(1, count, send_stats, 0)
    when(row >= 2, (relay_up,), "start")
    when(jnp.logical_not(bottom), up_, "wait_recv")
    when(row + 2 < rows, (relay_down,), "start")
    spread_row(4)
    for phase_col in range(2):
        upsample(((6, 3),), 0, phase_col, False)

    @pl.when(jnp.logical_not(bottom))
    def _():
        for phase_col in range(2):
            upsample(((5, 3),), 1, phase_col, False)

    def take_stats(k, carry):
        stat_wait(lax.rem(me + k, count)).wait_recv()
        return carry

    lax.fori_loop(1, count, take_stats, 0)

    sums = jnp.sum(stats[...], axis=0)
    parts = []
    for _ in range(3):
        parts.append(sums.astype(jnp.bfloat16))
        sums = sums - parts[-1].astype(jnp.float32)
    sums = jnp.dot(
        jnp.concatenate(parts, axis=0), same[...], preferred_element_type=jnp.float32
    )
    sums = sums[0:2] + sums[2:4] + sums[4:6]
    cells = 4 * height * breadth * count * width
    mean = sums[0:1] / cells
    spread = sums[1:2] / cells - mean * mean
    for n in range(4, 8):
        locals_[n].wait()
    scale = lax.rsqrt(spread + EPS) * gain[...]
    offset = shift[...] - mean * scale

    first_col = jnp.where(core == 0, 1, -1)
    last_col = jnp.where(core == cores - 1, breadth, span)
    even_in = (index >= first_col) & (index <= last_col)
    odd_in = (index > first_col) & (index <= last_col + 1)

    def lay(dst, r, even, odd, keep):
        slot = r % 2
        even = jnp.where(even_in & keep, even, 0.0)
        odd = jnp.where(odd_in & keep, odd, 0.0)
        hf[slot, 0, pl.ds(8, span)] = even
        hf[slot, 1, pl.ds(8, span)] = odd
        dst[r, :, pl.ds(0, cout)] = hf[slot, 0, pl.ds(7, span)].astype(jnp.bfloat16)
        dst[r, :, pl.ds(cout, cout)] = odd.astype(jnp.bfloat16)
        dst[r, :, pl.ds(2 * cout, cout)] = even.astype(jnp.bfloat16)
        dst[r, :, pl.ds(3 * cout, cout)] = hf[slot, 1, pl.ds(9, span)].astype(jnp.bfloat16)

    hf[:, :, pl.ds(0, 8)] = jnp.zeros((2, 2, 8, cout), jnp.float32)
    hf[:, :, pl.ds(8 + span, 8)] = jnp.zeros((2, 2, 8, cout), jnp.float32)

    def kept(r, low, high):
        keep = True
        if r < low:
            keep = jnp.logical_not(top)
        if r >= high:
            keep = jnp.logical_not(bottom)
        return keep

    def hide(r):
        even = silu(up[r, 0].astype(jnp.float32) * scale + offset)
        odd = silu(up[r, 1].astype(jnp.float32) * scale + offset)
        lay(hs, r, even, odd, kept(r, 2, 6))

    def convolve(src, lines, weight, bias):
        lhs = jnp.concatenate(
            [
                jnp.concatenate([src[r + a, :, pl.ds(low, 3 * cout)] for a in range(3)], axis=1)
                for r in lines
                for low in (cout, 0)
            ],
            axis=0,
        )
        total = jnp.dot(lhs, weight[...], preferred_element_type=jnp.float32) + bias[...]
        cut = lambda n: total[n * span : (n + 1) * span]
        return [(r, cut(2 * n), cut(2 * n + 1)) for n, r in enumerate(lines)]

    def first(lines):
        for r, even, odd in convolve(hs, lines, w1buf, b1):
            lay(acts, r, silu(even), silu(odd), kept(r, 1, 5))

    for n in range(1, 3):
        locals_[n + 1].wait()
        weights[n].wait_recv()
    for r in range(1, 7):
        hide(r)
    for r in range(1, 5):
        first((r,))

    when(row >= 2, (relay_down,), "wait_recv")
    when(row == 1, first_up, "wait_recv")
    when(row + 2 < rows, (relay_up,), "wait_recv")
    when(row == rows - 2, last_down, "wait_recv")
    spread_row(0)
    spread_row(5)
    for phase_col in range(2):
        upsample(((0, 0),), 0, phase_col, False)
        upsample(((7, 4),), 1, phase_col, False)
    hide(0)
    hide(7)
    first((0,))
    first((5,))

    sides.wait_send()
    for copy in weights:
        copy.wait_send()
    when(jnp.logical_not(bottom), down, "wait_send")
    when(bottom, last_down, "wait_send")
    when(jnp.logical_not(top), up_, "wait_send")
    when(top, first_up, "wait_send")
    when(row >= 2, (relay_up,), "wait_send")
    when(row + 2 < rows, (relay_down,), "wait_send")

    def drain(k, carry):
        stat_copy(k, lax.rem(me + k, count)).wait_send()
        return carry

    lax.fori_loop(1, count, drain, 0)


def finish(acts, w2buf, b2, out, mix, rows_out, out_sem):
    span = acts.shape[1]
    cout = w2buf.shape[1]
    breadth = span - EDGE
    copies = []
    for r in (1, 2, 0, 3):
        lhs = jnp.concatenate(
            [
                jnp.concatenate([acts[r + a, :, pl.ds(low, 3 * cout)] for a in range(3)], axis=1)
                for low in (cout, 0)
            ],
            axis=0,
        )
        total = jnp.dot(lhs, w2buf[...], preferred_element_type=jnp.float32) + b2[...]
        for lane in range(cout // 128):
            cut = slice(lane * 128, (lane + 1) * 128)
            mix[r % 2, lane, pl.ds(6, span, stride=2), :] = total[:span, cut]
            mix[r % 2, lane, pl.ds(5, span, stride=2), :] = total[span:, cut]
            rows_out[r, :, pl.ds(lane * 128, 128)] = mix[
                r % 2, lane, pl.ds(8, 2 * breadth), :
            ].astype(jnp.bfloat16)
        copies.append(pltpu.make_async_copy(rows_out.at[r], out.at[r], out_sem.at[r]))
        copies[-1].start()
    for copy in copies:
        copy.wait()


def local(rows, cores, image, dw, gain, shift, w1, b1, w2, b2):
    height, breadth, cin = image.shape
    half = dw.shape[3]
    cout = gain.shape[0]
    span = breadth + EDGE
    bf16, f32 = jnp.bfloat16, jnp.float32
    count = rows * cores
    vmem = pl.BlockSpec(memory_space=pltpu.VMEM)
    hbm = pl.BlockSpec(memory_space=pltpu.HBM)
    acts, w2_whole, b2_kept = pl.pallas_call(
        functools.partial(kernel, rows, cores),
        out_shape=(
            pltpu.VMEM((2 * height + 2, span, 4 * cout), bf16),
            pltpu.VMEM((9 * cout, cout), bf16),
            pltpu.VMEM((1, cout), f32),
        ),
        in_specs=[hbm] * 8,
        out_specs=(vmem, vmem, vmem),
        scratch_shapes=[
            pltpu.VMEM((1, cout), f32),
            pltpu.VMEM((1, cout), f32),
            pltpu.VMEM((1, cout), f32),
            pltpu.VMEM((3 * height, breadth + 2 * EDGE, cin), bf16),
            pltpu.VMEM((breadth + 2 * EDGE, cin), f32),
            pltpu.VMEM((3 * height, span, 2 * cin), bf16),
            pltpu.VMEM((16 * cin, cout), bf16),
            pltpu.VMEM((9 * cout, cout), bf16),
            pltpu.VMEM((2 * height + 4, 2, span, cout), bf16),
            pltpu.VMEM((2, 2, span + 16, cout), f32),
            pltpu.VMEM((2 * height + 4, span, 4 * cout), bf16),
            pltpu.VMEM((count, 2, cout), f32),
            pltpu.VMEM((cout, cout), bf16),
            pltpu.SemaphoreType.DMA((8,)),
            pltpu.SemaphoreType.DMA((14,)),
            pltpu.SemaphoreType.DMA((14,)),
            pltpu.SemaphoreType.DMA((count,)),
            pltpu.SemaphoreType.DMA((count,)),
            pltpu.SemaphoreType.REGULAR((max(rows.bit_length(), 1),)),
        ],
        compiler_params=pltpu.CompilerParams(
            collective_id=0, has_side_effects=True, vmem_limit_bytes=61 << 20
        ),
    )(
        image,
        dw.reshape(-1, half),
        gain.reshape(1, -1),
        shift.reshape(1, -1),
        w1.reshape(-1, half),
        b1.reshape(1, -1),
        w2.reshape(-1, half),
        b2.reshape(1, -1),
    )
    return pl.pallas_call(
        finish,
        out_shape=jax.ShapeDtypeStruct((2 * height, 2 * breadth, cout), bf16),
        in_specs=[vmem, vmem, vmem],
        out_specs=pl.BlockSpec(memory_space=pl.ANY),
        scratch_shapes=[
            pltpu.VMEM((2, cout // 128, 2 * span + 16, 128), f32),
            pltpu.VMEM((2 * height, 2 * breadth, cout), bf16),
            pltpu.SemaphoreType.DMA((2 * height,)),
        ],
        compiler_params=pltpu.CompilerParams(vmem_limit_bytes=16 << 20),
    )(acts, w2_whole, b2_kept)


def solution(mesh):
    placed = (
        P(("groups", "rows"), "fsdp", None),
        P(None, None, None, "fsdp"),
        P(),
        P(),
        P(None, None, None, "fsdp"),
        P(),
        P(None, None, None, "fsdp"),
        P(),
    )
    return jax.shard_map(
        functools.partial(local, mesh.shape["rows"], mesh.shape["fsdp"]),
        mesh=mesh,
        in_specs=placed,
        out_specs=P(("groups", "rows"), "fsdp", None),
        check_vma=False,
    )
```

```python
import functools

import jax
import jax.numpy as jnp
from jax import lax
from jax.experimental import pallas as pl
from jax.experimental.pallas import tpu as pltpu
from jax.sharding import PartitionSpec as P

NORM_GROUPS = 32
EPS = 1e-05
MESH = pl.DeviceIdType.MESH
EDGE = 16
TAPS = ((3, 1), (2, 0))


def silu(v):
    h = 0.5 * v
    return h + h * jnp.tanh(h)


def kernel(
    rows, cores,
    image, dw, gain_in, shift_in, w1, b1_in, w2, b2_in,
    acts, w2buf, b2,
    gain, shift, b1,
    xbuf, xf, xs, dwbuf, w1buf, up, hf, hs, stats, same,
    local_sem, send_sem, recv_sem, stat_send, stat_recv, ring,
):
    row, core = lax.axis_index("rows"), lax.axis_index("fsdp")
    other = cores - 1 - core
    count = rows * cores
    me = row * cores + core
    height, breadth, cin = image.shape
    cout = gain.shape[1]
    half = dw.shape[1]
    span = xs.shape[1]
    side = pl.multiple_of(other * (breadth - EDGE), EDGE)
    far = pl.multiple_of(core * (breadth + EDGE), EDGE)
    mine = pl.multiple_of(core * half, 128)

    locals_ = [
        pltpu.make_async_copy(
            image, xbuf.at[pl.ds(height, height), pl.ds(EDGE, breadth)], local_sem.at[0]
        ),
        pltpu.make_async_copy(dw, dwbuf.at[:, pl.ds(mine, half)], local_sem.at[1]),
        pltpu.make_async_copy(w1, w1buf.at[:, pl.ds(mine, half)], local_sem.at[2]),
        pltpu.make_async_copy(w2, w2buf.at[:, pl.ds(mine, half)], local_sem.at[3]),
        pltpu.make_async_copy(gain_in, gain, local_sem.at[4]),
        pltpu.make_async_copy(shift_in, shift, local_sem.at[5]),
        pltpu.make_async_copy(b1_in, b1, local_sem.at[6]),
        pltpu.make_async_copy(b2_in, b2, local_sem.at[7]),
    ]

    barrier = pltpu.get_barrier_semaphore()

    def signal(sem, to_row, to_core):
        pl.semaphore_signal(
            sem, inc=1, device_id={"rows": to_row, "fsdp": to_core}, device_id_type=MESH
        )

    def near(gap):
        return jnp.where(row >= gap, 1, 0) + jnp.where(row + gap < rows, 1, 0)

    def call(sem, gap, to_cores):
        for inside, to_row in ((row >= gap, row - gap), (row + gap < rows, row + gap)):
            @pl.when(inside)
            def _():
                for to_core in to_cores:
                    signal(sem, to_row, to_core)

    signal(barrier, row, other)
    call(barrier, 1, (core, other))
    for copy in locals_:
        copy.start()
    xbuf[:, pl.ds(far, EDGE), :] = jnp.zeros((xbuf.shape[0], EDGE, cin), xbuf.dtype)
    pl.semaphore_wait(barrier, 2 * near(1) + 1)

    def remote(src, dst, index, to_row, to_core):
        return pltpu.make_async_remote_copy(
            src_ref=src,
            dst_ref=dst,
            send_sem=send_sem.at[index],
            recv_sem=recv_sem.at[index],
            device_id={"rows": to_row, "fsdp": to_core},
            device_id_type=MESH,
        )

    def piece(src_row, dst_row, index, to_row, low, size):
        return remote(
            image.at[src_row, pl.ds(low, size)],
            xbuf.at[dst_row, pl.ds(EDGE + low, size)],
            index, to_row, core,
        )

    def corner(src_row, dst_row, index, to_row):
        return remote(
            image.at[src_row, pl.ds(side, EDGE)],
            xbuf.at[dst_row, pl.ds(far, EDGE)],
            index, to_row, other,
        )

    top, bottom = row == 0, row == rows - 1
    below = jnp.where(bottom, row - 1, row + 1)
    above = jnp.where(top, row + 1, row - 1)

    def line(src_row, dst_row, index, to_row, sizes):
        lows = [sum(sizes[:n]) for n in range(len(sizes))]
        return [
            piece(src_row, dst_row, index + 1 + n, to_row, low, size)
            for n, (low, size) in enumerate(zip(lows, sizes))
        ] + [corner(src_row, dst_row, index, to_row)]

    early = breadth // 2 // EDGE * EDGE
    whole, halves = (breadth,), (early, breadth - early)
    down, up_ = line(1, 1, 4, below, whole), line(0, 4, 6, above, halves)
    last_down, first_up = line(1, 5, 9, below, whole), line(0, 0, 11, above, halves)
    reach = pl.multiple_of(other * EDGE, EDGE)

    def pass_on(src_row, dst_row, index, to_row):
        line = pl.ds(reach, breadth + EDGE)
        return remote(xbuf.at[src_row, line], xbuf.at[dst_row, line], index, to_row, core)

    relay_up = pass_on(1, 5, 14, lax.rem(row + rows - 2, rows))
    relay_down = pass_on(4, 0, 15, lax.rem(row + 2, rows))
    sides = remote(
        image.at[:, pl.ds(side, EDGE)],
        xbuf.at[pl.ds(height, height), pl.ds(far, EDGE)],
        0, row, other,
    )
    weights = [
        remote(dw, dwbuf.at[:, pl.ds(mine, half)], 1, row, other),
        remote(w1, w1buf.at[:, pl.ds(mine, half)], 2, row, other),
        remote(w2, w2buf.at[:, pl.ds(mine, half)], 3, row, other),
    ]

    def when(condition, copies, what):
        @pl.when(condition)
        def _():
            for copy in copies:
                getattr(copy, what)()

    def send_down():
        when(jnp.logical_not(bottom), down, "start")
        when(bottom, last_down, "start")

    def send_up(part):
        when(jnp.logical_not(top), up_[part], "start")
        when(top, first_up[part], "start")

    send_down()
    sides.start()
    weights[0].start()
    weights[1].start()
    weights[2].start()

    gaps = []
    while (1 << len(gaps)) < rows:
        gaps.append(1 << len(gaps))

    def meet(turn):
        if turn:
            pl.semaphore_wait(ring.at[turn - 1], near(gaps[turn - 1]))
        if turn < len(gaps):
            call(ring.at[turn], gaps[turn], (core,))

    meet(0)

    @pl.when(row == 0)
    def _():
        xbuf[pl.ds(0, 2)] = jnp.zeros((2,) + xbuf.shape[1:], xbuf.dtype)

    @pl.when(row == rows - 1)
    def _():
        xbuf[pl.ds(4, 2)] = jnp.zeros((2,) + xbuf.shape[1:], xbuf.dtype)

    def spread_row(r):
        xf[...] = xbuf[r].astype(jnp.float32)
        xs[r, :, pl.ds(0, cin)] = xf[pl.ds(EDGE - 2, span), :].astype(jnp.bfloat16)
        xs[r, :, pl.ds(cin, cin)] = xf[pl.ds(EDGE - 1, span), :].astype(jnp.bfloat16)

    meet(1)
    locals_[0].wait()
    sides.wait_recv()
    spread_row(2)
    spread_row(3)

    index = lax.broadcasted_iota(jnp.int32, (span, 1), 0)

    def upsample(pairs, phase_row, phase_col, measure):
        lhs = jnp.concatenate(
            [jnp.concatenate([xs[i], xs[i + 1]], axis=1) for _, i in pairs], axis=0
        )
        rhs = jnp.concatenate(
            [
                dwbuf[pl.ds((TAPS[phase_row][dr] * 4 + TAPS[phase_col][dc]) * cin, cin), :]
                for dr in range(2)
                for dc in range(2)
            ],
            axis=0,
        )
        total = jnp.dot(lhs, rhs, preferred_element_type=jnp.float32).astype(jnp.bfloat16)
        for n, (o, _) in enumerate(pairs):
            block = total[n * span : (n + 1) * span]
            up[o, phase_col] = block
            if measure is not False:
                first = 1 + phase_col
                own = (index >= first) & (index < first + breadth) & measure
                v = jnp.where(own, block.astype(jnp.float32), 0.0)
                stats[me, 0:1] += jnp.sum(v, axis=0, keepdims=True)
                stats[me, 1:2] += jnp.sum(v * v, axis=0, keepdims=True)

    stats[me] = jnp.zeros(stats.shape[1:], stats.dtype)
    width = cout // NORM_GROUPS
    lane_a = lax.broadcasted_iota(jnp.int32, (cout, cout), 0) // width
    lane_b = lax.broadcasted_iota(jnp.int32, (cout, cout), 1) // width
    same[...] = jnp.where(lane_a == lane_b, 1.0, 0.0).astype(jnp.bfloat16)
    for turn in range(2, len(gaps)):
        meet(turn)
    send_up(slice(0, 1))
    locals_[1].wait()
    weights[0].wait_recv()
    for phase_col in range(2):
        upsample(((4, 2),), 0, phase_col, True)
        upsample(((3, 2),), 1, phase_col, True)

    @pl.when(bottom)
    def _():
        spread_row(4)
        for phase_col in range(2):
            upsample(((5, 3),), 1, phase_col, True)

    when(jnp.logical_not(top), down, "wait_recv")
    spread_row(1)
    for phase_col in range(2):
        upsample(((2, 1),), 0, phase_col, True)
        upsample(((1, 1),), 1, phase_col, jnp.logical_not(top))

    def stat_copy(slot, peer):
        return pltpu.make_async_remote_copy(
            src_ref=stats.at[me],
            dst_ref=stats.at[me],
            send_sem=stat_send.at[slot],
            recv_sem=stat_recv.at[me],
            device_id={"rows": lax.div(peer, cores), "fsdp": lax.rem(peer, cores)},
            device_id_type=MESH,
        )

    def stat_wait(peer):
        return pltpu.make_async_remote_copy(
            src_ref=stats.at[peer],
            dst_ref=stats.at[peer],
            send_sem=stat_send.at[0],
            recv_sem=stat_recv.at[peer],
            device_id={"rows": lax.div(peer, cores), "fsdp": lax.rem(peer, cores)},
            device_id_type=MESH,
        )

    def send_stats(k, carry):
        stat_copy(k, lax.rem(me + k, count)).start()
        return carry

    for turn in range(max(2, len(gaps)), len(gaps) + 1):
        meet(turn)
    lax.fori_loop(1, count, send_stats, 0)
    send_up(slice(1, 3))
    when(row >= 2, (relay_up,), "start")
    when(jnp.logical_not(bottom), up_, "wait_recv")
    when(row + 2 < rows, (relay_down,), "start")
    spread_row(4)
    for phase_col in range(2):
        upsample(((6, 3),), 0, phase_col, False)

    @pl.when(jnp.logical_not(bottom))
    def _():
        for phase_col in range(2):
            upsample(((5, 3),), 1, phase_col, False)

    def take_stats(k, carry):
        stat_wait(lax.rem(me + k, count)).wait_recv()
        return carry

    lax.fori_loop(1, count, take_stats, 0)

    sums = jnp.sum(stats[...], axis=0)
    parts = []
    for _ in range(3):
        parts.append(sums.astype(jnp.bfloat16))
        sums = sums - parts[-1].astype(jnp.float32)
    sums = jnp.dot(
        jnp.concatenate(parts, axis=0), same[...], preferred_element_type=jnp.float32
    )
    sums = sums[0:2] + sums[2:4] + sums[4:6]
    cells = 4 * height * breadth * count * width
    mean = sums[0:1] / cells
    spread = sums[1:2] / cells - mean * mean
    for n in range(4, 8):
        locals_[n].wait()
    scale = lax.rsqrt(spread + EPS) * gain[...]
    offset = shift[...] - mean * scale

    first_col = jnp.where(core == 0, 1, -1)
    last_col = jnp.where(core == cores - 1, breadth, span)
    even_in = (index >= first_col) & (index <= last_col)
    odd_in = (index > first_col) & (index <= last_col + 1)

    def lay(dst, r, even, odd, keep):
        slot = r % 2
        even = jnp.where(even_in & keep, even, 0.0)
        odd = jnp.where(odd_in & keep, odd, 0.0)
        hf[slot, 0, pl.ds(8, span)] = even
        hf[slot, 1, pl.ds(8, span)] = odd
        dst[r, :, pl.ds(0, cout)] = hf[slot, 0, pl.ds(7, span)].astype(jnp.bfloat16)
        dst[r, :, pl.ds(cout, cout)] = odd.astype(jnp.bfloat16)
        dst[r, :, pl.ds(2 * cout, cout)] = even.astype(jnp.bfloat16)
        dst[r, :, pl.ds(3 * cout, cout)] = hf[slot, 1, pl.ds(9, span)].astype(jnp.bfloat16)

    hf[:, :, pl.ds(0, 8)] = jnp.zeros((2, 2, 8, cout), jnp.float32)
    hf[:, :, pl.ds(8 + span, 8)] = jnp.zeros((2, 2, 8, cout), jnp.float32)

    def kept(r, low, high):
        keep = True
        if r < low:
            keep = jnp.logical_not(top)
        if r >= high:
            keep = jnp.logical_not(bottom)
        return keep

    def hide(r):
        even = silu(up[r, 0].astype(jnp.float32) * scale + offset)
        odd = silu(up[r, 1].astype(jnp.float32) * scale + offset)
        lay(hs, r, even, odd, kept(r, 2, 6))

    def convolve(src, lines, weight, bias):
        lhs = jnp.concatenate(
            [
                jnp.concatenate([src[r + a, :, pl.ds(low, 3 * cout)] for a in range(3)], axis=1)
                for r in lines
                for low in (cout, 0)
            ],
            axis=0,
        )
        total = jnp.dot(lhs, weight[...], preferred_element_type=jnp.float32) + bias[...]
        cut = lambda n: total[n * span : (n + 1) * span]
        return [(r, cut(2 * n), cut(2 * n + 1)) for n, r in enumerate(lines)]

    def first(lines):
        for r, even, odd in convolve(hs, lines, w1buf, b1):
            lay(acts, r, silu(even), silu(odd), kept(r, 1, 5))

    for n in range(1, 3):
        locals_[n + 1].wait()
        weights[n].wait_recv()
    for r in range(1, 7):
        hide(r)
    for r in range(1, 5):
        first((r,))

    when(row >= 2, (relay_down,), "wait_recv")
    when(row == 1, first_up, "wait_recv")
    when(row + 2 < rows, (relay_up,), "wait_recv")
    when(row == rows - 2, last_down, "wait_recv")
    spread_row(0)
    spread_row(5)
    for phase_col in range(2):
        upsample(((0, 0),), 0, phase_col, False)
        upsample(((7, 4),), 1, phase_col, False)
    hide(0)
    hide(7)
    first((0,))
    first((5,))

    sides.wait_send()
    for copy in weights:
        copy.wait_send()
    when(jnp.logical_not(bottom), down, "wait_send")
    when(bottom, last_down, "wait_send")
    when(jnp.logical_not(top), up_, "wait_send")
    when(top, first_up, "wait_send")
    when(row >= 2, (relay_up,), "wait_send")
    when(row + 2 < rows, (relay_down,), "wait_send")

    def drain(k, carry):
        stat_copy(k, lax.rem(me + k, count)).wait_send()
        return carry

    lax.fori_loop(1, count, drain, 0)


def finish(acts, w2buf, b2, out, mix, rows_out, out_sem):
    span = acts.shape[1]
    cout = w2buf.shape[1]
    breadth = span - EDGE
    copies = []
    for r in (1, 2, 0, 3):
        lhs = jnp.concatenate(
            [
                jnp.concatenate([acts[r + a, :, pl.ds(low, 3 * cout)] for a in range(3)], axis=1)
                for low in (cout, 0)
            ],
            axis=0,
        )
        total = jnp.dot(lhs, w2buf[...], preferred_element_type=jnp.float32) + b2[...]
        for lane in range(cout // 128):
            cut = slice(lane * 128, (lane + 1) * 128)
            mix[r % 2, lane, pl.ds(6, span, stride=2), :] = total[:span, cut]
            mix[r % 2, lane, pl.ds(5, span, stride=2), :] = total[span:, cut]
            rows_out[r, :, pl.ds(lane * 128, 128)] = mix[
                r % 2, lane, pl.ds(8, 2 * breadth), :
            ].astype(jnp.bfloat16)
        copies.append(pltpu.make_async_copy(rows_out.at[r], out.at[r], out_sem.at[r]))
        copies[-1].start()
    for copy in copies:
        copy.wait()


def local(rows, cores, image, dw, gain, shift, w1, b1, w2, b2):
    height, breadth, cin = image.shape
    half = dw.shape[3]
    cout = gain.shape[0]
    span = breadth + EDGE
    bf16, f32 = jnp.bfloat16, jnp.float32
    count = rows * cores
    vmem = pl.BlockSpec(memory_space=pltpu.VMEM)
    hbm = pl.BlockSpec(memory_space=pltpu.HBM)
    acts, w2_whole, b2_kept = pl.pallas_call(
        functools.partial(kernel, rows, cores),
        out_shape=(
            pltpu.VMEM((2 * height + 2, span, 4 * cout), bf16),
            pltpu.VMEM((9 * cout, cout), bf16),
            pltpu.VMEM((1, cout), f32),
        ),
        in_specs=[hbm] * 8,
        out_specs=(vmem, vmem, vmem),
        scratch_shapes=[
            pltpu.VMEM((1, cout), f32),
            pltpu.VMEM((1, cout), f32),
            pltpu.VMEM((1, cout), f32),
            pltpu.VMEM((3 * height, breadth + 2 * EDGE, cin), bf16),
            pltpu.VMEM((breadth + 2 * EDGE, cin), f32),
            pltpu.VMEM((3 * height, span, 2 * cin), bf16),
            pltpu.VMEM((16 * cin, cout), bf16),
            pltpu.VMEM((9 * cout, cout), bf16),
            pltpu.VMEM((2 * height + 4, 2, span, cout), bf16),
            pltpu.VMEM((2, 2, span + 16, cout), f32),
            pltpu.VMEM((2 * height + 4, span, 4 * cout), bf16),
            pltpu.VMEM((count, 2, cout), f32),
            pltpu.VMEM((cout, cout), bf16),
            pltpu.SemaphoreType.DMA((8,)),
            pltpu.SemaphoreType.DMA((16,)),
            pltpu.SemaphoreType.DMA((16,)),
            pltpu.SemaphoreType.DMA((count,)),
            pltpu.SemaphoreType.DMA((count,)),
            pltpu.SemaphoreType.REGULAR((max(rows.bit_length(), 1),)),
        ],
        compiler_params=pltpu.CompilerParams(
            collective_id=0, has_side_effects=True, vmem_limit_bytes=61 << 20
        ),
    )(
        image,
        dw.reshape(-1, half),
        gain.reshape(1, -1),
        shift.reshape(1, -1),
        w1.reshape(-1, half),
        b1.reshape(1, -1),
        w2.reshape(-1, half),
        b2.reshape(1, -1),
    )
    return pl.pallas_call(
        finish,
        out_shape=jax.ShapeDtypeStruct((2 * height, 2 * breadth, cout), bf16),
        in_specs=[vmem, vmem, vmem],
        out_specs=pl.BlockSpec(memory_space=pl.ANY),
        scratch_shapes=[
            pltpu.VMEM((2, cout // 128, 2 * span + 16, 128), f32),
            pltpu.VMEM((2 * height, 2 * breadth, cout), bf16),
            pltpu.SemaphoreType.DMA((2 * height,)),
        ],
        compiler_params=pltpu.CompilerParams(vmem_limit_bytes=16 << 20),
    )(acts, w2_whole, b2_kept)


def solution(mesh):
    placed = (
        P(("groups", "rows"), "fsdp", None),
        P(None, None, None, "fsdp"),
        P(),
        P(),
        P(None, None, None, "fsdp"),
        P(),
        P(None, None, None, "fsdp"),
        P(),
    )
    return jax.shard_map(
        functools.partial(local, mesh.shape["rows"], mesh.shape["fsdp"]),
        mesh=mesh,
        in_specs=placed,
        out_specs=P(("groups", "rows"), "fsdp", None),
        check_vma=False,
    )
```
